512 devices in a mesh: rep: 16 (over y, core), dom: 32 (over x, z).
Axes of the slice: x: 4, y: 8, z: 8, core: 2. Of those that a mesh axis runs over, the one named last changes fastest.
Arguments:
- features: bfloat16 [524288, 768], P(('rep', 'dom')), may hold values from -24 to 24
- cotangent: bfloat16 [524288, 1024], P(('rep', 'dom')), may hold values from -0.008239746 to 0.008239746
- w_self: bfloat16 [768, 1024], P('dom'), may hold values from -0.21875 to 0.21875
- w_neigh: bfloat16 [768, 1024], P('dom'), may hold values from -0.21875 to 0.21875
- tile_vals: bfloat16 [16384, 128, 128], P(('rep', 'dom')), may hold values from 0 to 0.088378906
- tile_src: int32 [16384], P(('rep', 'dom')), may hold values from 0 to 7
- tile_peer: int32 [16384], P(('rep', 'dom')), may hold values from 0 to 31
- in_block: int32 [16384], P(('rep', 'dom')), may hold values from 0 to 7
Outputs:
- grad_self: float32 [768, 1024], P('dom')
- grad_neigh: float32 [768, 1024], P('dom')
The draws below stay inside these ranges and needn't reach their ends.
Inputs may be any that keep to these rules, and one draw needn't show every extreme that they name: `in_block`: all tiles that one partition sends to one receiving partition land in the same receiver block.
All inputs are finite; a program needn't handle non-finite values.
Results may differ from the reference program's by a relative error of at most 0.023.
Values may be sent and summed in bfloat16 or wider, within the bound.
A program may use at most 128 MiB of HBM per device.

```python
import math
import jax
import jax.numpy as jnp
import numpy as np
from jax import lax

F = 768
H = 1024
BLK = 128
BLK_DEV = 8
TILE_DEV = 32
ROWS_DEV = 1024
NODES = 32768
TILES = 1024
N_REP = 16
N_DOM = 32


def touch_ends(array, key, least, largest):
    shape = array.shape
    index_at = [jax.random.randint(jax.random.fold_in(key, axis), (), 0, shape[axis]) for axis in range(len(shape))]
    array = array.at[tuple(index_at)].set(least)
    longest = shape.index(max(shape))
    index_at[longest] = (index_at[longest] + 1) % shape[longest]
    return array.at[tuple(index_at)].set(largest)


def raised(entries, own_key, source, target, shards_of, factor):
    def block_of(position):
        return (jnp.arange(entries.shape[position]) // (entries.shape[position] // shards_of)).reshape((-1,) + (1,) * (entries.ndim - 1 - position))

    first = jax.random.permutation(own_key, shards_of)[block_of(target)]
    other_side = (block_of(target) + shards_of // 2) % shards_of
    return jnp.where((block_of(source) == first) | (block_of(source) == other_side), factor * entries, entries)


def level_of(stream_key, shape, cuts, smallest, top_value):
    def one(axis_at, parts):
        draws = jax.random.uniform(jax.random.fold_in(jax.random.fold_in(stream_key, 6), axis_at), (parts,), jnp.float32, smallest / len(cuts), top_value / len(cuts))
        return jnp.repeat(jnp.exp(draws), shape[axis_at] // parts).reshape((-1,) + (1,) * (len(shape) - axis_at - 1))

    loudness = one(*cuts[0])
    for cut in cuts[1:]:
        loudness = loudness * one(*cut)
    return loudness


def rank_table(amount, skew):
    portions = [(1 << 20) // math.isqrt(grade ** skew) + 1 for grade in range(1, amount + 1)]
    spread = 1 + sum(portions) // (1 << 30)
    return np.cumsum(np.array([max(1, weight // spread) for weight in portions]))


def ranked(stream_key, shape, amount, lean):
    listing = rank_table(amount, lean)
    ticket = jax.random.randint(jax.random.fold_in(stream_key, 1), shape, 0, int(listing[amount - 1]))
    grade = jnp.searchsorted(jnp.asarray(listing, jnp.int32), ticket, side="right")
    return jax.random.permutation(jax.random.fold_in(stream_key, 2), amount)[grade].astype(jnp.int32)


def bell_draw(own_key, shape, width, bound, split=(), held_as=jnp.bfloat16):
    drawn = jax.random.normal(own_key, shape, jnp.float32) * width
    if len(split) > 0:
        drawn = level_of(own_key, shape, split, -0.22, 0.18) * drawn
    return jnp.clip(drawn, min=-bound, max=bound).astype(held_as)


def heavy_noise(key, shape, deviation, reach, split, heavy, held_as=jnp.bfloat16):
    array = deviation * jax.random.normal(key, shape, jnp.float32)
    if split:
        array = array * level_of(key, shape, split, -0.22, 0.18)
    return jnp.clip(raised(array, jax.random.fold_in(key, 3), *heavy), -reach, reach).astype(held_as)


def setup_inputs(seed: int = 0) -> dict:
    seeds = jax.random.split(jax.random.key(seed), 9)
    return {
        "features": heavy_noise(seeds[0], (N_REP * NODES, F), 1.0, 24.0, ((0, 512),), (0, 1, 256, 6.0)),
        "cotangent": bell_draw(seeds[1], (N_REP * NODES, H), (1.0 / (N_REP * N_DOM * BLK * BLK_DEV) ** 0.5), 0.008239746, ((0, 512),)),
        "w_self": bell_draw(seeds[2], (F, H), F ** -0.5, 0.21875, ((0, 32),)),
        "w_neigh": bell_draw(seeds[3], (F, H), F ** -0.5, 0.21875, ((0, 32),)),
        "tile_vals": jnp.clip(0.088378906 * jax.random.uniform(seeds[4], (N_REP * TILES, BLK, BLK), jnp.float32) ** level_of(seeds[4], (N_REP * TILES, BLK, BLK), ((0, 512),), -0.2, 0.2), 0.0, 0.088378906).astype(jnp.bfloat16),
        "tile_src": touch_ends(jax.random.randint(seeds[5], (N_REP * TILES,), 0, BLK_DEV), jax.random.fold_in(seeds[5], 1), 0, BLK_DEV - 1).astype(jnp.int32),
        "tile_peer": touch_ends(ranked(seeds[6], (N_REP * TILES,), N_DOM, 2), jax.random.fold_in(seeds[6], 3), 0, N_DOM - 1).astype(jnp.int32),
        "in_block": touch_ends(jax.random.randint(seeds[7], (N_REP * N_DOM * N_DOM,), 0, BLK_DEV), jax.random.fold_in(seeds[7], 1), 0, BLK_DEV - 1).astype(jnp.int32),
    }


def gelu_tanh(value):
    return jax.nn.gelu(value, approximate=True)

def reference(features, cotangent, w_self, w_neigh, tile_vals, tile_src, tile_peer, in_block):
    rows = N_DOM * ROWS_DEV
    tile_total = N_DOM * TILE_DEV
    grad_total = jnp.zeros((F, 2 * H), jnp.float32)
    for replica in range(N_REP):
        feats = features[replica * rows:(replica + 1) * rows]
        blocks = feats.reshape(N_DOM, BLK_DEV, BLK, F)
        tiles = tile_vals[replica * tile_total:(replica + 1) * tile_total].reshape(N_DOM, TILE_DEV, BLK, BLK)
        sources = tile_src[replica * tile_total:(replica + 1) * tile_total].reshape(N_DOM, TILE_DEV)
        peers = tile_peer[replica * tile_total:(replica + 1) * tile_total].reshape(N_DOM, TILE_DEV)
        targets = in_block[replica * N_DOM * N_DOM:(replica + 1) * N_DOM * N_DOM].reshape(N_DOM, N_DOM)
        receivers = jnp.arange(N_DOM, dtype=jnp.int32)

        def add_source(total, sender):
            own = blocks[sender]
            picked = own[sources[sender]]
            product = jnp.einsum('tij,tjf->tif', tiles[sender].astype(jnp.float32), picked.astype(jnp.float32))
            slots = jnp.zeros((N_DOM, BLK, F), jnp.float32).at[peers[sender]].add(product)
            sent = lax.optimization_barrier(slots.astype(jnp.bfloat16)).astype(jnp.float32)
            total = total.at[receivers, targets[:, sender]].add(sent)
            return (total, None)
        start = jnp.zeros((N_DOM, BLK_DEV, BLK, F), jnp.float32)
        aggregate, _ = lax.scan(add_source, start, jnp.arange(N_DOM, dtype=jnp.int32))
        aggregate = aggregate.reshape(rows, F).astype(jnp.bfloat16)
        preact = jnp.dot(feats, w_self, preferred_element_type=jnp.float32) + jnp.dot(aggregate, w_neigh, preferred_element_type=jnp.float32)
        cot = cotangent[replica * rows:(replica + 1) * rows].astype(jnp.float32)
        _, pull = jax.vjp(gelu_tanh, preact)
        grad_pre = pull(cot)[0].astype(jnp.bfloat16)
        feats32 = feats.astype(jnp.float32).reshape(N_DOM, ROWS_DEV, F)
        agg32 = aggregate.astype(jnp.float32).reshape(N_DOM, ROWS_DEV, F)
        pre32 = grad_pre.astype(jnp.float32).reshape(N_DOM, ROWS_DEV, H)
        terms = jnp.concatenate([jnp.einsum('dnf,dnh->dfh', feats32, pre32), jnp.einsum('dnf,dnh->dfh', agg32, pre32)], axis=2)
        rounded = lax.optimization_barrier(terms.astype(jnp.bfloat16)).astype(jnp.float32)
        grad_total = grad_total + lax.optimization_barrier(jnp.sum(rounded, axis=0))
    return (grad_total[:, :H], grad_total[:, H:])
```

```python
import functools

import jax
import jax.numpy as jnp
from jax import lax
from jax.experimental import pallas as pl
from jax.experimental.pallas import tpu as pltpu
from jax.sharding import Mesh
from jax.sharding import PartitionSpec as P

AXES = ("y", "c", "x", "z")
SIZES = (8, 2, 4, 8)
NY, NC, NX, NZ = SIZES
NDOM = NX * NZ
MESH = pl.DeviceIdType.MESH
VMEM_BYTES = 60 * 1024 * 1024
F32 = jnp.float32
BF16 = jnp.bfloat16

DIST = (4, 3, 3, 2, 2, 1, 1)
ITEMS = []
for _i, _d in enumerate(DIST):
    ITEMS += [(_i % 2, _d), (1 - _i % 2, -_d)]
ITEMS += [(0, 0), (1, 0)]


def position():
    return tuple(lax.axis_index(a) for a in AXES)


def moved(me, axis, by):
    return tuple(
        lax.rem(m + (by % SIZES[axis]), SIZES[axis]) if a == axis else m
        for a, m in enumerate(me)
    )


def greet(me):
    barrier = pltpu.get_barrier_semaphore()
    count = 0
    for axis, size in enumerate(SIZES):
        for by in range(1, size):
            pl.semaphore_signal(
                barrier, inc=1, device_id=moved(me, axis, by), device_id_type=MESH
            )
            count += 1
    pl.semaphore_wait(barrier, count)


def remote(src, dst, send, recv, target):
    return pltpu.make_async_remote_copy(
        src_ref=src, dst_ref=dst, send_sem=send, recv_sem=recv,
        device_id=target, device_id_type=MESH,
    )


def slots_kernel(src, peer, feats, tiles, out, acc):
    half = acc.shape[2] // 2
    block = acc.shape[1]

    def clear(p, _):
        acc[p] = jnp.zeros(acc.shape[1:], F32)
        return 0

    lax.fori_loop(0, acc.shape[0], clear, 0)

    def tile(t, _):
        rows = pl.ds(pl.multiple_of(src[t] * block, block), block)
        acc[peer[t]] += jnp.dot(tiles[t], feats[rows, :], preferred_element_type=F32)
        return 0

    lax.fori_loop(0, tiles.shape[0], tile, 0)

    def put(p, _):
        out[0, p] = acc[p, :, :half].astype(BF16)
        out[1, p] = acc[p, :, half:].astype(BF16)
        return 0

    lax.fori_loop(0, acc.shape[0], put, 0)


def make_slots(features, tile_vals, tile_src, tile_peer):
    block = tile_vals.shape[1]
    width = features.shape[1]
    vmem = pl.BlockSpec(memory_space=pltpu.VMEM)
    smem = pl.BlockSpec(memory_space=pltpu.SMEM)
    return pl.pallas_call(
        slots_kernel,
        out_shape=jax.ShapeDtypeStruct((2, NDOM, block, width // 2), BF16),
        in_specs=[smem, smem, vmem, vmem],
        out_specs=vmem,
        scratch_shapes=[pltpu.VMEM((NDOM, block, width), F32)],
        compiler_params=pltpu.CompilerParams(vmem_limit_bytes=VMEM_BYTES),
        name="slots",
    )(tile_src, tile_peer, features, tile_vals)


def exchange_kernel(
    slots, ib, w, agg, wg,
    xb, zr, zs, ibs,
    x_send, x_recv, x_own, z_send, z_recv, ib_send, ib_recv, ib_own,
    wa_send, wa_recv, w_own, wb_send, wb_recv, wc_send, wc_recv, wd_send, wd_recv,
):
    me = position()
    y, c, x, z = me
    block, half = xb.shape[2], xb.shape[3]
    blocks = zr.shape[2]
    rows = 32
    greet(me)

    def at_z(by):
        return lax.rem(z + (by % NZ), NZ)

    def at_x(by):
        return lax.rem(x + (by % NX), NX)

    def at_y(by):
        return lax.rem(y + (by % NY), NY)

    ib_local = pltpu.make_async_copy(ib, ibs.at[z], ib_own)
    ib_local.start()
    own_w = pltpu.make_async_copy(w.at[c, y], wg.at[c, y, x * NZ + z], w_own)
    own_w.start()

    def ib_copy(by):
        return remote(ib, ibs.at[z], ib_send.at[by - 1], ib_recv.at[by - 1], moved(me, 3, by))

    def ib_arrival(by):
        return remote(ib, ibs.at[at_z(-by)], ib_send.at[by - 1], ib_recv.at[by - 1], me)

    def wa_copy(by):
        dst = wg.at[c, y, x * NZ + z]
        return remote(w.at[c, y], dst, wa_send.at[by - 1], wa_recv.at[by - 1], moved(me, 3, by))

    def wa_arrival(by):
        dst = wg.at[c, y, x * NZ + at_z(-by)]
        return remote(w.at[c, y], dst, wa_send.at[by - 1], wa_recv.at[by - 1], me)

    def wb_ref(at):
        return wg.at[c, y, pl.ds(at * NZ, NZ)]

    def wb_copy(by):
        return remote(wb_ref(x), wb_ref(x), wb_send.at[by - 1], wb_recv.at[by - 1], moved(me, 2, by))

    def wb_arrival(by):
        dst = wb_ref(at_x(-by))
        return remote(wb_ref(x), dst, wb_send.at[by - 1], wb_recv.at[by - 1], me)

    def wc_copy(by):
        ref = wg.at[c, y]
        return remote(ref, ref, wc_send.at[by - 1], wc_recv.at[by - 1], moved(me, 0, by))

    def wc_arrival(by):
        dst = wg.at[c, at_y(-by)]
        return remote(wg.at[c, y], dst, wc_send.at[by - 1], wc_recv.at[by - 1], me)

    wd_copy = remote(wg.at[c], wg.at[c], wd_send, wd_recv, moved(me, 1, 1))
    wd_arrival = remote(wg.at[1 - c], wg.at[1 - c], wd_send, wd_recv, me)

    def x_copy(j, by):
        h, rel = ITEMS[j]
        src = slots.at[h, at_x(by) * NZ + at_z(rel)]
        return remote(src, xb.at[j, x], x_send.at[j, by - 1], x_recv.at[j, by - 1], moved(me, 2, by))

    def x_arrival(j, by):
        h, rel = ITEMS[j]
        src = slots.at[h, x * NZ + at_z(rel)]
        return remote(src, xb.at[j, at_x(-by)], x_send.at[j, by - 1], x_recv.at[j, by - 1], me)

    def x_local(j):
        h, rel = ITEMS[j]
        return pltpu.make_async_copy(slots.at[h, x * NZ + at_z(rel)], xb.at[j, x], x_own.at[j])

    def x_start(j):
        for by in (2, 1, 3):
            x_copy(j, by).start()
        x_local(j).start()

    def x_wait(j):
        x_local(j).wait()
        for by in (2, 1, 3):
            x_arrival(j, by).wait_recv()

    def z_refs(d, i):
        if i < 2:
            return xb.at[2 * i + d], zr.at[d, i, pl.ds(0, NX)]
        return zs.at[d, i - 2], zr.at[d, i]

    def z_copy(d, i):
        src, dst = z_refs(d, i)
        return remote(src, dst, z_send.at[d, i], z_recv.at[d, i], moved(me, 3, 1 - 2 * d))

    def z_arrival(d, i):
        src, dst = z_refs(d, i)
        return remote(src, dst, z_send.at[d, i], z_recv.at[d, i], me)

    def placed(at_dest, at_sender, piece, k, r):
        total = None
        for xs in range(NX):
            mine = ibs[at_dest, pl.ds(xs * NZ + at_sender, 1), :] == k
            term = jnp.where(mine, piece(xs)[pl.ds(r, rows), :].astype(F32), 0.0)
            total = term if total is None else total + term
        return total

    def each_part(body):
        def step(n, _):
            k = n // (block // rows)
            r = pl.multiple_of(lax.rem(n, block // rows) * rows, rows)
            body(k, r)
            return 0

        lax.fori_loop(0, blocks * (block // rows), step, 0)

    def combine(d, i):
        sign = 1 - 2 * d
        dest = at_z(sign * DIST[i])

        def body(k, r):
            total = placed(dest, z, lambda xs: xb.at[2 * i + d, xs], k, r)
            if i < 4:
                total += placed(dest, at_z(-sign), lambda xs: zr.at[d, i - 2, xs], k, r)
            else:
                total += zr[d, i - 2, k, pl.ds(r, rows), :].astype(F32)
            zs[d, i - 2, k, pl.ds(r, rows), :] = total.astype(BF16)

        each_part(body)

    for by in range(1, NZ):
        ib_copy(by).start()
    for j in range(4):
        x_start(j)
    own_w.wait()
    for by in range(1, NZ):
        wa_copy(by).start()
    for j in range(4, 6):
        x_start(j)
    ib_local.wait()
    for by in range(1, NZ):
        ib_arrival(by).wait_recv()

    for i in range(len(DIST)):
        for d in (0, 1):
            x_wait(2 * i + d)
            if i >= 2:
                z_arrival(d, i - 2).wait_recv()
                combine(d, i)
            if i < 2:
                z_copy(d, i).start()
        if i >= 2:
            for d in (0, 1):
                z_copy(d, i).start()
        if 2 * i + 7 < len(ITEMS):
            x_start(2 * i + 6)
            x_start(2 * i + 7)
        if i == 0:
            for by in range(1, NZ):
                wa_arrival(by).wait_recv()
            for by in range(1, NX):
                wb_copy(by).start()
        if i == 1:
            for by in range(1, NX):
                wb_arrival(by).wait_recv()
            for by in range(1, NY):
                wc_copy(by).start()
        if i == 5:
            for by in range(1, NY):
                wc_arrival(by).wait_recv()
            wd_copy.start()

    last = len(DIST)
    x_wait(2 * last)
    x_wait(2 * last + 1)
    for i in (5, 6):
        for d in (0, 1):
            z_arrival(d, i).wait_recv()

    for h in (0, 1):
        i_plus = 6 if h == 0 else 5
        i_minus = 5 if h == 0 else 6

        def body(k, r, h=h, i_plus=i_plus, i_minus=i_minus):
            total = placed(z, z, lambda xs: xb.at[2 * last + h, xs], k, r)
            total += zr[0, i_plus, k, pl.ds(r, rows), :].astype(F32)
            total += zr[1, i_minus, k, pl.ds(r, rows), :].astype(F32)
            at = pl.multiple_of(k * block + r, rows)
            agg[pl.ds(at, rows), h * half:(h + 1) * half] = total.astype(BF16)

        each_part(body)

    wd_arrival.wait_recv()
    wd_copy.wait_send()
    for by in range(1, NZ):
        ib_copy(by).wait_send()
        wa_copy(by).wait_send()
    for by in range(1, NX):
        wb_copy(by).wait_send()
    for by in range(1, NY):
        wc_copy(by).wait_send()
    for j in range(len(ITEMS)):
        for by in range(1, NX):
            x_copy(j, by).wait_send()
    for i in range(len(DIST)):
        for d in (0, 1):
            z_copy(d, i).wait_send()


def exchange(slots, ib, w):
    _, _, block, half = slots.shape
    blocks = 8
    dma = pltpu.SemaphoreType.DMA
    vmem = pl.BlockSpec(memory_space=pltpu.VMEM)
    anywhere = pl.BlockSpec(memory_space=pl.ANY)
    steps = len(DIST)
    return pl.pallas_call(
        exchange_kernel,
        out_shape=(
            jax.ShapeDtypeStruct((blocks * block, 2 * half), BF16),
            jax.ShapeDtypeStruct((NC, NY, NDOM, *w.shape[2:]), BF16),
        ),
        in_specs=[anywhere, vmem, anywhere],
        out_specs=(vmem, anywhere),
        scratch_shapes=[
            pltpu.VMEM((len(ITEMS), NX, block, half), BF16),
            pltpu.VMEM((2, steps, blocks, block, half), BF16),
            pltpu.VMEM((2, steps - 2, blocks, block, half), BF16),
            pltpu.VMEM((NZ, *ib.shape), jnp.int32),
            dma((len(ITEMS), NX - 1)),
            dma((len(ITEMS), NX - 1)),
            dma((len(ITEMS),)),
            dma((2, steps)),
            dma((2, steps)),
            dma((NZ - 1,)),
            dma((NZ - 1,)),
            dma,
            dma((NZ - 1,)),
            dma((NZ - 1,)),
            dma,
            dma((NX - 1,)),
            dma((NX - 1,)),
            dma((NY - 1,)),
            dma((NY - 1,)),
            dma,
            dma,
        ],
        compiler_params=pltpu.CompilerParams(
            collective_id=0, has_side_effects=True, vmem_limit_bytes=VMEM_BYTES
        ),
        name="exchange",
    )(slots, ib, w)


def terms_kernel(feats, agg, cot, wg, t0, t1, t2, left):
    rows = feats.shape[0]
    per = wg.shape[1]
    chunk = wg.shape[3]

    @pl.when(pl.program_id(0) == 0)
    def _():
        left[0] = feats[...].T
        left[1] = agg[...].T

    def weights(side):
        return jnp.concatenate([wg[side, n] for n in range(per)], axis=1)

    pre = jnp.dot(feats[...], weights(0), preferred_element_type=F32)
    pre += jnp.dot(agg[...], weights(1), preferred_element_type=F32)
    scale = 0.7978845608
    square = pre * pre
    t = jnp.tanh(scale * (pre + 0.044715 * (square * pre)))
    slope = 0.5 * (1.0 + t) + (0.5 * scale) * pre * (1.0 - t * t) * (1.0 + 0.134145 * square)
    grad = (cot[...].astype(F32) * slope).astype(BF16)
    for side in range(NC):
        both = jnp.dot(left[side], grad, preferred_element_type=F32)
        for n in range(per):
            v = both[:, n * chunk:(n + 1) * chunk].reshape(NX, NZ, 3, 8, chunk)
            for xs in range(NX):
                t0[side, n, :, xs] = v[xs, :, 0].astype(BF16)
                t1[side, :, n, xs] = v[xs, :, 1].astype(BF16)
                t2[side, xs, :, n] = v[xs, :, 2].astype(BF16)


def make_terms(features, agg, cotangent, wg):
    rows, width = features.shape
    chunk = wg.shape[3]
    per = 2
    whole = pl.BlockSpec((rows, width), lambda q: (0, 0))
    tile = (8, chunk)
    return pl.pallas_call(
        terms_kernel,
        grid=(NY // per,),
        out_shape=(
            jax.ShapeDtypeStruct((NC, NY, NZ, NX, *tile), BF16),
            jax.ShapeDtypeStruct((NC, NZ, NY, NX, *tile), BF16),
            jax.ShapeDtypeStruct((NC, NX, NZ, NY, *tile), BF16),
        ),
        in_specs=[
            whole,
            whole,
            pl.BlockSpec((rows, per * chunk), lambda q: (0, q)),
            pl.BlockSpec((NC, per, width, chunk), lambda q: (0, q, 0, 0)),
        ],
        out_specs=(
            pl.BlockSpec((NC, per, NZ, NX, *tile), lambda q: (0, q, 0, 0, 0, 0)),
            pl.BlockSpec((NC, NZ, per, NX, *tile), lambda q: (0, 0, q, 0, 0, 0)),
            pl.BlockSpec((NC, NX, NZ, per, *tile), lambda q: (0, 0, 0, q, 0, 0)),
        ),
        scratch_shapes=[pltpu.VMEM((2, width, rows), BF16)],
        compiler_params=pltpu.CompilerParams(vmem_limit_bytes=VMEM_BYTES),
        name="terms",
    )(features, agg, cotangent, wg)


ORDER = ((0, 3, 2), (3, 0, 2), (2, 3, 0))


def reduce_kernel(
    t0, t1, t2, out_self, out_neigh,
    own0, own1, own2, got0, got1, got2, mid0, mid1, mid2, low0, low1, low2,
    a0, a1, a2, b0, b1, b2, d0, d1, d2, every,
    own_sem, c_send, c_recv, s_send, s_recv, g_send, g_recv, p_send, p_recv,
):
    me = position()
    y, c = me[0], me[1]
    given = (t0, t1, t2)
    got = (got0, got1, got2)
    parts = ((own0, own1, own2), (mid0, mid1, mid2), (low0, low1, low2))
    inbox = ((a0, a1, a2), (b0, b1, b2), (d0, d1, d2))
    own = parts[0]
    greet(me)

    def load(j):
        return pltpu.make_async_copy(given[j].at[c], own[j], own_sem.at[j])

    def to_partner(j, target):
        return remote(given[j].at[1 - c], got[j], c_send.at[j], c_recv.at[j], target)

    for j in range(3):
        to_partner(j, moved(me, 1, 1)).start()
        load(j).start()

    def hop(j, s, by, arriving=False):
        axis = ORDER[j][s]
        size = SIZES[axis]
        here = me[axis]
        src = parts[s][j].at[lax.rem(here + by, size)]
        send, recv = s_send.at[s, j, by - 1], s_recv.at[s, j, by - 1]
        if arriving:
            return remote(src, inbox[s][j].at[lax.rem(here + size - by, size)], send, recv, me)
        return remote(src, inbox[s][j].at[here], send, recv, moved(me, axis, by))

    def hops(j, s):
        return range(1, SIZES[ORDER[j][s]])

    for j in range(3):
        load(j).wait()
        to_partner(j, me).wait_recv()
        n1, n2 = own[j].shape[:2]

        def add(n, _, j=j, n2=n2):
            a, b = n // n2, lax.rem(n, n2)
            own[j][a, b] = (own[j][a, b].astype(F32) + got[j][a, b].astype(F32)).astype(BF16)
            return 0

        lax.fori_loop(0, n1 * n2, add, 0)
        for by in hops(j, 0):
            hop(j, 0, by).start()

    for s in range(3):
        for j in range(3):
            axis = ORDER[j][s]
            size = SIZES[axis]
            here = me[axis]
            for by in hops(j, s):
                hop(j, s, by, arriving=True).wait_recv()

            def total(at, j=j, s=s, here=here, size=size):
                out = parts[s][j][(here, *at)].astype(F32)
                for by in range(1, size):
                    out += inbox[s][j][(lax.rem(here + by, size), *at)].astype(F32)
                return out

            if s == 2:
                every[c, y, j] = total(())
                continue

            def add(n, _, j=j, s=s, total=total):
                parts[s + 1][j][n] = total((n,)).astype(BF16)
                return 0

            lax.fori_loop(0, parts[s + 1][j].shape[0], add, 0)
            for by in hops(j, s + 1):
                hop(j, s + 1, by).start()

    def gather(by, arriving=False):
        dst = every.at[c, lax.rem(y + NY - by, NY) if arriving else y]
        target = me if arriving else moved(me, 0, by)
        return remote(every.at[c, y], dst, g_send.at[by - 1], g_recv.at[by - 1], target)

    for by in range(1, NY):
        gather(by).start()
    for by in range(1, NY):
        gather(by, arriving=True).wait_recv()
    pair = remote(every.at[c], every.at[c], p_send, p_recv, moved(me, 1, 1))
    pair.start()
    remote(every.at[c], every.at[1 - c], p_send, p_recv, me).wait_recv()
    for side, out in ((0, out_self), (1, out_neigh)):
        for n in range(NY):
            for j in range(3):
                out[j * 8:(j + 1) * 8, n * 128:(n + 1) * 128] = every[side, n, j]
    pair.wait_send()
    for by in range(1, NY):
        gather(by).wait_send()
    for j in range(3):
        to_partner(j, moved(me, 1, 1)).wait_send()
        for s in range(3):
            for by in hops(j, s):
                hop(j, s, by).wait_send()


def reduce_terms(terms):
    dma = pltpu.SemaphoreType.DMA
    shapes = [t.shape[1:] for t in terms]
    tile = shapes[0][-2:]
    vmem = pl.BlockSpec(memory_space=pltpu.VMEM)
    scratch = [pltpu.VMEM(s[skip:], BF16) for skip in (0, 0, 1, 2) for s in shapes]
    scratch += [pltpu.VMEM(s[skip:], BF16) for skip in (0, 1, 2) for s in shapes]
    out = jax.ShapeDtypeStruct((3 * tile[0], NY * tile[1]), F32)
    return pl.pallas_call(
        reduce_kernel,
        out_shape=(out, out),
        in_specs=[pl.BlockSpec(memory_space=pl.ANY)] * 3,
        out_specs=(vmem, vmem),
        scratch_shapes=scratch
        + [
            pltpu.VMEM((NC, NY, 3, *tile), F32),
            dma((3,)),
            dma((3,)),
            dma((3,)),
            dma((3, 3, 7)),
            dma((3, 3, 7)),
            dma((NY - 1,)),
            dma((NY - 1,)),
            dma,
            dma,
        ],
        compiler_params=pltpu.CompilerParams(
            collective_id=1, has_side_effects=True, vmem_limit_bytes=VMEM_BYTES
        ),
        name="reduce",
    )(*terms)


def shards(features, cotangent, w_self, w_neigh, tile_vals, tile_src, tile_peer, in_block):
    half = features.shape[1] // 2
    own_rows, hidden = w_self.shape
    chunk = hidden // NY
    w = jnp.stack([w_self, w_neigh]).reshape(NC, own_rows, NY, chunk).transpose(0, 2, 1, 3)
    ib = jnp.broadcast_to(in_block[:, None], (NDOM, half))
    slots = make_slots(features, tile_vals, tile_src, tile_peer)
    agg, wg = exchange(slots, ib, w)
    wg = wg.reshape(NC, NY, NDOM * own_rows, chunk)
    terms = make_terms(features, agg, cotangent, wg)
    return reduce_terms(terms)


def solution(mesh):
    split = Mesh(mesh.devices.reshape(SIZES), AXES)
    every = P(AXES)
    rows = P(AXES, None)
    placed = (
        rows,
        rows,
        P(("x", "z"), None),
        P(("x", "z"), None),
        P(AXES, None, None),
        every,
        every,
        every,
    )
    out = P(("x", "z"), None)
    return jax.shard_map(
        shards, mesh=split, in_specs=placed, out_specs=(out, out), check_vma=False
    )
```

```python
import functools

import jax
import jax.numpy as jnp
from jax import lax
from jax.experimental import pallas as pl
from jax.experimental.pallas import tpu as pltpu
from jax.sharding import Mesh
from jax.sharding import PartitionSpec as P

AXES = ("y", "c", "x", "z")
SIZES = (8, 2, 4, 8)
NY, NC, NX, NZ = SIZES
NDOM = NX * NZ
MESH = pl.DeviceIdType.MESH
VMEM_BYTES = 67043328
F32 = jnp.float32
BF16 = jnp.bfloat16

DIST = (4, 3, 3, 2, 2, 1, 1)
ITEMS = []
for _i, _d in enumerate(DIST):
    ITEMS += [(_i % 2, _d), (1 - _i % 2, -_d)]
ITEMS += [(0, 0), (1, 0)]


def position():
    return tuple(lax.axis_index(a) for a in AXES)


def moved(me, axis, by):
    return tuple(
        lax.rem(m + (by % SIZES[axis]), SIZES[axis]) if a == axis else m
        for a, m in enumerate(me)
    )


def greet(me):
    barrier = pltpu.get_barrier_semaphore()
    count = 0
    for axis, size in enumerate(SIZES):
        for by in range(1, size):
            pl.semaphore_signal(
                barrier, inc=1, device_id=moved(me, axis, by), device_id_type=MESH
            )
            count += 1
    pl.semaphore_wait(barrier, count)


def remote(src, dst, send, recv, target):
    return pltpu.make_async_remote_copy(
        src_ref=src, dst_ref=dst, send_sem=send, recv_sem=recv,
        device_id=target, device_id_type=MESH,
    )


ORDER = ((0, 3, 2), (3, 0, 2), (2, 3, 0))


def step_kernel(
    idx, inb, tiles, feats, cot_in, w_self, w_neigh, out, wg,
    ct, sl, xb, zr, zs, ibs, cot, w, pre_own, agg, left, grad,
    out0, out1, out2, own0, own1, own2, got0, got1, got2, mid0, mid1, mid2, low0, low1, low2,
    a0, a1, a2, b0, b1, b2, d0, d1, d2, every,
    x_send, x_recv, z_send, z_recv, ib_send, ib_recv, cot_sem, w_sem,
    wa_send, wa_recv, w_own, wb_send, wb_recv, wc_send, wc_recv, wd_send, wd_recv,
    c_send, c_recv, s_send, s_recv, g_send, g_recv, p_send, p_recv,
):
    me = position()
    y, c, x, z = me
    block, half = xb.shape[2], xb.shape[3]
    blocks = zr.shape[2]
    owned = w_self.shape[0]
    chunk = wg.shape[3]
    count = tiles.shape[0]
    rows = 32
    last = len(DIST)
    final = last - 1
    groups = z_send.shape[1] - final
    per = blocks // groups

    def at_z(by):
        return lax.rem(z + (by % NZ), NZ)

    def at_x(by):
        return lax.rem(x + (by % NX), NX)

    def at_y(by):
        return lax.rem(y + (by % NY), NY)

    for s in range(NDOM):
        ibs[z, s:s + 1, :] = jnp.full((1, half), inb[s], jnp.int32)
    load_cot = pltpu.make_async_copy(cot_in, cot, cot_sem)
    load_cot.start()
    ct[...] = jnp.zeros_like(ct)

    def chain(t, _):
        ct[t] = tiles[t].astype(F32) + ct[idx[t]]
        return 0

    lax.fori_loop(0, count, chain, 0)

    def slots(rel):
        j0, j1 = (
            next(j for j, (h, at) in enumerate(ITEMS) if h == side and (at - rel) % NZ == 0)
            for side in (0, 1)
        )

        def one(by, _):
            p = lax.rem(x + by, NX) * NZ + at_z(rel)
            parts = [ct[idx[count + p * blocks + b]].astype(BF16) for b in range(blocks)]
            value = jnp.dot(jnp.concatenate(parts, axis=1), feats[...], preferred_element_type=F32)
            sl[j0, by] = value[:, :half].astype(BF16)
            sl[j1, by] = value[:, half:].astype(BF16)
            return 0

        lax.fori_loop(0, NX, one, 0)
        xb[j0, x] = sl[j0, 0]
        xb[j1, x] = sl[j1, 0]

    slots(4)
    greet(me)

    def ib_copy(by):
        ref = ibs.at[z]
        return remote(ref, ref, ib_send.at[by - 1], ib_recv.at[by - 1], moved(me, 3, by))

    def ib_arrival(by):
        return remote(ibs.at[z], ibs.at[at_z(-by)], ib_send.at[by - 1], ib_recv.at[by - 1], me)

    def wg_rows(at, size):
        return wg.at[c, y, pl.ds(pl.multiple_of(at * owned, owned), size * owned)]

    def w_src(ref):
        return ref.at[:, pl.ds(pl.multiple_of(y * chunk, chunk), chunk)]

    def w_local(ref):
        return pltpu.make_async_copy(w_src(ref), wg_rows(x * NZ + z, 1), w_own)

    def wa_copy(ref, by):
        dst = wg_rows(x * NZ + z, 1)
        return remote(w_src(ref), dst, wa_send.at[by - 1], wa_recv.at[by - 1], moved(me, 3, by))

    def wa_arrival(by):
        dst = wg_rows(x * NZ + at_z(-by), 1)
        return remote(w_src(w_self), dst, wa_send.at[by - 1], wa_recv.at[by - 1], me)

    def wb_copy(by):
        ref = wg_rows(x * NZ, NZ)
        return remote(ref, ref, wb_send.at[by - 1], wb_recv.at[by - 1], moved(me, 2, by))

    def wb_arrival(by):
        dst = wg_rows(at_x(-by) * NZ, NZ)
        return remote(wg_rows(x * NZ, NZ), dst, wb_send.at[by - 1], wb_recv.at[by - 1], me)

    def wc_copy(by):
        ref = wg.at[c, y]
        return remote(ref, ref, wc_send.at[by - 1], wc_recv.at[by - 1], moved(me, 0, by))

    def wc_arrival(by):
        dst = wg.at[c, at_y(-by)]
        return remote(wg.at[c, y], dst, wc_send.at[by - 1], wc_recv.at[by - 1], me)

    wd_copy = remote(wg.at[c], wg.at[c], wd_send, wd_recv, moved(me, 1, 1))
    wd_arrival = remote(wg.at[1 - c], wg.at[1 - c], wd_send, wd_recv, me)
    load_w = pltpu.make_async_copy(wg, w, w_sem)

    def x_copy(j, by, arriving=False):
        send, recv = x_send.at[j, by - 1], x_recv.at[j, by - 1]
        if arriving:
            return remote(sl.at[j, by], xb.at[j, at_x(-by)], send, recv, me)
        return remote(sl.at[j, by], xb.at[j, x], send, recv, moved(me, 2, by))

    def x_start(j):
        for by in (2, 1, 3):
            x_copy(j, by).start()

    def x_wait(j):
        for by in (2, 1, 3):
            x_copy(j, by, arriving=True).wait_recv()

    def z_copy(d, i, g=0, arriving=False):
        if i < 2:
            src, dst = xb.at[2 * i + d], zr.at[d, i, pl.ds(0, NX)]
        elif i < final:
            src, dst = zs.at[d, i - 2], zr.at[d, i]
        else:
            piece = pl.ds(g * per, per)
            src, dst = zs.at[d, i - 2, piece], zr.at[d, i, piece]
        target = me if arriving else moved(me, 3, 1 - 2 * d)
        return remote(src, dst, z_send.at[d, i + g], z_recv.at[d, i + g], target)

    def pieces(i):
        return range(groups if i == final else 1)

    def placed(at_dest, at_sender, piece, k, r):
        total = None
        for xs in range(NX):
            mine = ibs[at_dest, pl.ds(xs * NZ + at_sender, 1), :] == k
            term = jnp.where(mine, piece(xs)[pl.ds(r, rows), :].astype(F32), 0.0)
            total = term if total is None else total + term
        return total

    def each_part(first, number, body):
        def step(n, _):
            k = first + n // (block // rows)
            r = pl.multiple_of(lax.rem(n, block // rows) * rows, rows)
            body(k, r)
            return 0

        lax.fori_loop(0, number * (block // rows), step, 0)

    def combine(d, i):
        sign = 1 - 2 * d
        dest = at_z(sign * DIST[i])

        def body(k, r):
            total = placed(dest, z, lambda xs: xb.at[2 * i + d, xs], k, r)
            if i < 4:
                total += placed(dest, at_z(-sign), lambda xs: zr.at[d, i - 2, xs], k, r)
            else:
                total += zr[d, i - 2, k, pl.ds(r, rows), :].astype(F32)
            zs[d, i - 2, k, pl.ds(r, rows), :] = total.astype(BF16)

        each_part(0, blocks, body)

    def transpose_feats():
        def one(n, _):
            at = pl.ds(pl.multiple_of(n * block, block), block)
            left[0, :, at] = feats[at, :].T
            return 0

        lax.fori_loop(0, blocks, one, 0)

    def own_product():
        def one(n, _):
            both = jnp.concatenate([w[0, 2 * n], w[0, 2 * n + 1]], axis=1)
            value = jnp.dot(feats[...], both, preferred_element_type=F32)
            pre_own[n] = value
            return 0

        lax.fori_loop(0, NY // 2, one, 0)

    for j in range(2):
        x_start(j)
    for by in range(1, NZ):
        ib_copy(by).start()
    for side, ref in ((0, w_self), (1, w_neigh)):

        @pl.when(c == side)
        def _(ref=ref):
            w_local(ref).start()
            for by in range(1, NZ):
                wa_copy(ref, by).start()

    slots(3)
    slots(-3)
    for j in range(2, 4):
        x_start(j)

    for i in range(last):
        for d in (0, 1):
            x_wait(2 * i + d)
            if i >= 2:
                z_copy(d, i - 2, arriving=True).wait_recv()
                combine(d, i)
            if i < 2:
                z_copy(d, i).start()
        if i >= 2:
            for g in pieces(i):
                for d in (0, 1):
                    z_copy(d, i, g).start()
        if 2 * i + 5 < len(ITEMS):
            x_start(2 * i + 4)
            x_start(2 * i + 5)
        if i == 0:
            slots(2)
            slots(-2)
            w_local(w_self).wait()
            for by in range(1, NZ):
                wa_copy(w_self, by).wait_send()
                wa_arrival(by).wait_recv()
            for by in range(1, NX):
                wb_copy(by).start()
            for by in range(1, NZ):
                ib_arrival(by).wait_recv()
        if i == 1:
            slots(1)
            slots(-1)
            slots(0)
            for by in range(1, NX):
                wb_arrival(by).wait_recv()
            for by in range(1, NY):
                wc_copy(by).start()
        if i == 2:
            transpose_feats()
        if i == 4:
            for by in range(1, NY):
                wc_arrival(by).wait_recv()
            wd_copy.start()
        if i == 5:
            wd_arrival.wait_recv()
            load_w.start()
            load_w.wait()
            own_product()

    load_cot.wait()
    x_wait(2 * last)
    x_wait(2 * last + 1)
    for d in (0, 1):
        z_copy(d, final - 1, arriving=True).wait_recv()

    span = per * block
    scale = 0.7978845608
    for g in range(groups):
        for d in (0, 1):
            z_copy(d, final, g, arriving=True).wait_recv()
        for h in (0, 1):

            def body(k, r, h=h):
                total = placed(z, z, lambda xs: xb.at[2 * last + h, xs], k, r)
                total += zr[h, final, k, pl.ds(r, rows), :].astype(F32)
                total += zr[1 - h, final - 1, k, pl.ds(r, rows), :].astype(F32)
                at = pl.multiple_of((k - g * per) * block + r, rows)
                agg[pl.ds(at, rows), h * half:(h + 1) * half] = total.astype(BF16)

            each_part(g * per, per, body)
        here = pl.ds(g * span, span)
        left[1, :, here] = agg[...].T

        def gradient(n, _, here=here):
            both = jnp.concatenate([w[1, 2 * n], w[1, 2 * n + 1]], axis=1)
            pre = pre_own[n, here, :]
            pre += jnp.dot(agg[...], both, preferred_element_type=F32)
            square = pre * pre
            t = jnp.tanh(scale * (pre + 0.044715 * (square * pre)))
            slope = 0.5 * (1.0 + t)
            slope += (0.5 * scale) * pre * (1.0 - t * t) * (1.0 + 0.134145 * square)
            columns = pl.ds(pl.multiple_of(n * 2 * chunk, 2 * chunk), 2 * chunk)
            grad[n, here, :] = (cot[here, columns].astype(F32) * slope).astype(BF16)
            return 0

        lax.fori_loop(0, NY // 2, gradient, 0)

    own = (own0, own1, own2)
    outgoing = (out0, out1, out2)
    got = (got0, got1, got2)
    parts = (own, (mid0, mid1, mid2), (low0, low1, low2))
    inbox = ((a0, a1, a2), (b0, b1, b2), (d0, d1, d2))

    def terms(side, n, to):
        both = jnp.dot(left[side], grad[n], preferred_element_type=F32)
        for e in range(2):
            v = both[:, e * chunk:(e + 1) * chunk].reshape(NX, NZ, 3, 8, chunk)
            for xs in range(NX):
                to[0][2 * n + e, :, xs] = v[xs, :, 0].astype(BF16)
                to[1][:, 2 * n + e, xs] = v[xs, :, 1].astype(BF16)
                to[2][xs, :, 2 * n + e] = v[xs, :, 2].astype(BF16)

    def to_partner(j, n, target):
        at = pl.ds(2 * n, 2)
        if j == 0:
            src, dst = out0.at[at], got0.at[at]
        elif j == 1:
            src, dst = out1.at[:, at], got1.at[:, at]
        else:
            src, dst = out2.at[:, :, at], got2.at[:, :, at]
        return remote(src, dst, c_send.at[j, n], c_recv.at[j, n], target)

    for n in range(NY // 2):
        terms(1 - c, n, outgoing)
        for j in range(3):
            to_partner(j, n, moved(me, 1, 1)).start()

    def own_terms(n, _):
        terms(c, n, own)
        return 0

    lax.fori_loop(0, NY // 2, own_terms, 0)

    def hop(j, s, by, arriving=False):
        axis = ORDER[j][s]
        size = SIZES[axis]
        at = me[axis]
        src = parts[s][j].at[lax.rem(at + by, size)]
        send, recv = s_send.at[s, j, by - 1], s_recv.at[s, j, by - 1]
        if arriving:
            return remote(src, inbox[s][j].at[lax.rem(at + size - by, size)], send, recv, me)
        return remote(src, inbox[s][j].at[at], send, recv, moved(me, axis, by))

    def hops(j, s):
        return range(1, SIZES[ORDER[j][s]])

    for j in range(3):
        for n in range(NY // 2):
            to_partner(j, n, me).wait_recv()
        n1, n2 = own[j].shape[:2]

        def add(n, _, j=j, n2=n2):
            a, b = n // n2, lax.rem(n, n2)
            own[j][a, b] = (own[j][a, b].astype(F32) + got[j][a, b].astype(F32)).astype(BF16)
            return 0

        lax.fori_loop(0, n1 * n2, add, 0)
        for by in hops(j, 0):
            hop(j, 0, by).start()

    for s in range(3):
        for j in range(3):
            axis = ORDER[j][s]
            size = SIZES[axis]
            at_axis = me[axis]
            for by in hops(j, s):
                hop(j, s, by, arriving=True).wait_recv()

            def total(at, j=j, s=s, at_axis=at_axis, size=size):
                value = parts[s][j][(at_axis, *at)].astype(F32)
                for by in range(1, size):
                    value += inbox[s][j][(lax.rem(at_axis + by, size), *at)].astype(F32)
                return value

            if s == 2:
                every[c, y, j] = total(()).astype(BF16)
                continue

            def add(n, _, j=j, s=s, total=total):
                parts[s + 1][j][n] = total((n,)).astype(BF16)
                return 0

            lax.fori_loop(0, parts[s + 1][j].shape[0], add, 0)
            for by in hops(j, s + 1):
                hop(j, s + 1, by).start()

    def gather(by, arriving=False):
        dst = every.at[c, at_y(-by) if arriving else y]
        target = me if arriving else moved(me, 0, by)
        return remote(every.at[c, y], dst, g_send.at[by - 1], g_recv.at[by - 1], target)

    for by in range(1, NY):
        gather(by).start()
    for by in range(1, NY):
        gather(by, arriving=True).wait_recv()
    pair = remote(every.at[c], every.at[c], p_send, p_recv, moved(me, 1, 1))
    pair.start()
    remote(every.at[c], every.at[1 - c], p_send, p_recv, me).wait_recv()
    for side in (0, 1):
        for n in range(NY):
            for j in range(3):
                out[side, j * 8:(j + 1) * 8, n * chunk:(n + 1) * chunk] = every[side, n, j].astype(F32)

    pair.wait_send()
    wd_copy.wait_send()
    for by in range(1, NZ):
        ib_copy(by).wait_send()
    for by in range(1, NX):
        wb_copy(by).wait_send()
    for by in range(1, NY):
        wc_copy(by).wait_send()
        gather(by).wait_send()
    for j in range(len(ITEMS)):
        for by in range(1, NX):
            x_copy(j, by).wait_send()
    for i in range(last):
        for d in (0, 1):
            for g in pieces(i):
                z_copy(d, i, g).wait_send()
    for j in range(3):
        for n in range(NY // 2):
            to_partner(j, n, moved(me, 1, 1)).wait_send()
        for s in range(3):
            for by in hops(j, s):
                hop(j, s, by).wait_send()


def shards(features, cotangent, w_self, w_neigh, tile_vals, tile_src, tile_peer, in_block):
    count, block, _ = tile_vals.shape
    nodes, width = features.shape
    half = width // 2
    owned, hidden = w_self.shape
    blocks = nodes // block
    chunk = hidden // NY

    key = tile_peer * blocks + tile_src
    order = jnp.arange(count, dtype=jnp.int32)
    wanted = jnp.concatenate([key, jnp.arange(NDOM * blocks, dtype=jnp.int32)])
    limit = jnp.concatenate([order, jnp.full((NDOM * blocks,), count, jnp.int32)])
    found = (wanted[:, None] == key[None, :]) & (order[None, :] < limit[:, None])
    idx = jnp.max(jnp.where(found, order[None, :], -1), axis=1)
    idx = jnp.where(idx < 0, count, idx)

    dma = pltpu.SemaphoreType.DMA
    vmem = pl.BlockSpec(memory_space=pltpu.VMEM)
    smem = pl.BlockSpec(memory_space=pltpu.SMEM)
    anywhere = pl.BlockSpec(memory_space=pl.ANY)
    steps = len(DIST)
    items = len(ITEMS)
    groups = 4
    thirds = [(NY, NZ, NX, 8, chunk), (NZ, NY, NX, 8, chunk), (NX, NZ, NY, 8, chunk)]
    scratch = [
        pltpu.VMEM((count + 1, block, block), F32),
        pltpu.VMEM((items, NX, block, half), BF16),
        pltpu.VMEM((items, NX, block, half), BF16),
        pltpu.VMEM((2, steps, blocks, block, half), BF16),
        pltpu.VMEM((2, steps - 2, blocks, block, half), BF16),
        pltpu.VMEM((NZ, NDOM, half), jnp.int32),
        pltpu.VMEM((nodes, hidden), BF16),
        pltpu.VMEM((NC, NY, width, chunk), BF16),
        pltpu.VMEM((NY // 2, nodes, 2 * chunk), F32),
        pltpu.VMEM((nodes // groups, width), BF16),
        pltpu.VMEM((2, width, nodes), BF16),
        pltpu.VMEM((NY // 2, nodes, 2 * chunk), BF16),
    ]
    for skip in (0, 0, 0, 1, 2, 0, 1, 2):
        scratch += [pltpu.VMEM(t[skip:], BF16) for t in thirds]
    scratch += [
        pltpu.VMEM((NC, NY, 3, 8, chunk), BF16),
        dma((items, NX - 1)),
        dma((items, NX - 1)),
        dma((2, steps - 1 + groups)),
        dma((2, steps - 1 + groups)),
        dma((NZ - 1,)),
        dma((NZ - 1,)),
        dma,
        dma,
        dma((NZ - 1,)),
        dma((NZ - 1,)),
        dma,
        dma((NX - 1,)),
        dma((NX - 1,)),
        dma((NY - 1,)),
        dma((NY - 1,)),
        dma,
        dma,
        dma((3, NY // 2)),
        dma((3, NY // 2)),
        dma((3, 3, 7)),
        dma((3, 3, 7)),
        dma((NY - 1,)),
        dma((NY - 1,)),
        dma,
        dma,
    ]
    out, _ = pl.pallas_call(
        step_kernel,
        out_shape=(
            jax.ShapeDtypeStruct((NC, owned, hidden), F32),
            jax.ShapeDtypeStruct((NC, NY, width, chunk), BF16),
        ),
        in_specs=[smem, smem, vmem, vmem, anywhere, anywhere, anywhere],
        out_specs=(vmem, anywhere),
        scratch_shapes=scratch,
        compiler_params=pltpu.CompilerParams(
            collective_id=0, has_side_effects=True, vmem_limit_bytes=VMEM_BYTES
        ),
        name="step",
    )(idx, in_block, tile_vals, features, cotangent, w_self, w_neigh)
    return out[0], out[1]


def solution(mesh):
    split = Mesh(mesh.devices.reshape(SIZES), AXES)
    every = P(AXES)
    rows = P(AXES, None)
    placed = (
        rows,
        rows,
        P(("x", "z"), None),
        P(("x", "z"), None),
        P(AXES, None, None),
        every,
        every,
        every,
    )
    out = P(("x", "z"), None)
    return jax.shard_map(
        shards, mesh=split, in_specs=placed, out_specs=(out, out), check_vma=False
    )
```

```python
import functools

import jax
import jax.numpy as jnp
from jax import lax
from jax.experimental import pallas as pl
from jax.experimental.pallas import tpu as pltpu
from jax.sharding import Mesh
from jax.sharding import PartitionSpec as P

AXES = ("y", "c", "x", "z")
SIZES = (8, 2, 4, 8)
NY, NC, NX, NZ = SIZES
NDOM = NX * NZ
MESH = pl.DeviceIdType.MESH
VMEM_BYTES = 67043328
F32 = jnp.float32
BF16 = jnp.bfloat16

DIST = (4, 3, 3, 2, 2, 1, 1)
PIECES = ((0, 2), (2, 2), (4, 2), (6, 1), (7, 1))
Z_SEM = (0, 4, 8, 9, 10, 11, 12)
ITEMS = []
for _i, _d in enumerate(DIST):
    ITEMS += [(_i % 2, _d), (1 - _i % 2, -_d)]
ITEMS += [(0, 0), (1, 0)]


def position():
    return tuple(lax.axis_index(a) for a in AXES)


def moved(me, axis, by):
    return tuple(
        lax.rem(m + (by % SIZES[axis]), SIZES[axis]) if a == axis else m
        for a, m in enumerate(me)
    )


def greet(me):
    barrier = pltpu.get_barrier_semaphore()
    count = 0
    for axis, size in enumerate(SIZES):
        for by in range(1, size):
            pl.semaphore_signal(
                barrier, inc=1, device_id=moved(me, axis, by), device_id_type=MESH
            )
            count += 1
    for by in range(1, NY):
        other = moved(moved(me, 0, by), 1, 1)
        pl.semaphore_signal(barrier, inc=1, device_id=other, device_id_type=MESH)
        count += 1
    pl.semaphore_wait(barrier, count)


def remote(src, dst, send, recv, target):
    return pltpu.make_async_remote_copy(
        src_ref=src, dst_ref=dst, send_sem=send, recv_sem=recv,
        device_id=target, device_id_type=MESH,
    )


ORDER = ((0, 3, 2), (3, 0, 2), (2, 3, 0))


def step_kernel(
    idx, inb, tiles, feats, cot_in, w_self, w_neigh, out, wg,
    ct, sl, xb, zr, zs, ibs, cot, w, pre_own, agg, left, grad,
    lp, gp, own0, own1, own2, mid0, mid1, mid2, low0, low1, low2,
    a0, a1, a2, b0, b1, b2, d0, d1, d2, every,
    x_send, x_recv, z_send, z_recv, ib_send, ib_recv, cot_sem, w_sem,
    wa_send, wa_recv, w_own, wb_send, wb_recv, wc_send, wc_recv, wd_send, wd_recv,
    l_send, l_recv, c_send, c_recv, f_send, f_recv, s_send, s_recv, g_send, g_recv,
):
    me = position()
    y, c, x, z = me
    block, half = xb.shape[2], xb.shape[3]
    blocks = zr.shape[2]
    owned = w_self.shape[0]
    chunk = wg.shape[3]
    count = tiles.shape[0]
    rows = 32
    last = len(DIST)
    final = last - 1

    def at_z(by):
        return lax.rem(z + (by % NZ), NZ)

    def at_x(by):
        return lax.rem(x + (by % NX), NX)

    def at_y(by):
        return lax.rem(y + (by % NY), NY)

    for s in range(NDOM):
        ibs[z, s:s + 1, :] = jnp.full((1, half), inb[s], jnp.int32)
    load_cot = pltpu.make_async_copy(cot_in, cot, cot_sem)
    load_cot.start()
    ct[...] = jnp.zeros_like(ct)

    def chain(t, _):
        ct[t] = tiles[t].astype(F32) + ct[idx[t]]
        return 0

    lax.fori_loop(0, count, chain, 0)

    def slots(rel):
        j0, j1 = (
            next(j for j, (h, at) in enumerate(ITEMS) if h == side and (at - rel) % NZ == 0)
            for side in (0, 1)
        )

        def one(by, _):
            p = lax.rem(x + by, NX) * NZ + at_z(rel)
            parts = [ct[idx[count + p * blocks + b]].astype(BF16) for b in range(blocks)]
            value = jnp.dot(jnp.concatenate(parts, axis=1), feats[...], preferred_element_type=F32)
            sl[j0, by] = value[:, :half].astype(BF16)
            sl[j1, by] = value[:, half:].astype(BF16)
            return 0

        lax.fori_loop(0, NX, one, 0)
        xb[j0, x] = sl[j0, 0]
        xb[j1, x] = sl[j1, 0]

    slots(4)
    greet(me)

    def ib_copy(by):
        ref = ibs.at[z]
        return remote(ref, ref, ib_send.at[by - 1], ib_recv.at[by - 1], moved(me, 3, by))

    def ib_arrival(by):
        return remote(ibs.at[z], ibs.at[at_z(-by)], ib_send.at[by - 1], ib_recv.at[by - 1], me)

    def wg_rows(at, size):
        return wg.at[c, y, pl.ds(pl.multiple_of(at * owned, owned), size * owned)]

    def w_src(ref):
        return ref.at[:, pl.ds(pl.multiple_of(y * chunk, chunk), chunk)]

    def w_local(ref):
        return pltpu.make_async_copy(w_src(ref), wg_rows(x * NZ + z, 1), w_own)

    def wa_copy(ref, by):
        dst = wg_rows(x * NZ + z, 1)
        return remote(w_src(ref), dst, wa_send.at[by - 1], wa_recv.at[by - 1], moved(me, 3, by))

    def wa_arrival(by):
        dst = wg_rows(x * NZ + at_z(-by), 1)
        return remote(w_src(w_self), dst, wa_send.at[by - 1], wa_recv.at[by - 1], me)

    def wb_copy(by):
        ref = wg_rows(x * NZ, NZ)
        return remote(ref, ref, wb_send.at[by - 1], wb_recv.at[by - 1], moved(me, 2, by))

    def wb_arrival(by):
        dst = wg_rows(at_x(-by) * NZ, NZ)
        return remote(wg_rows(x * NZ, NZ), dst, wb_send.at[by - 1], wb_recv.at[by - 1], me)

    def wc_copy(by):
        ref = wg.at[c, y]
        return remote(ref, ref, wc_send.at[by - 1], wc_recv.at[by - 1], moved(me, 0, by))

    def wc_arrival(by):
        dst = wg.at[c, at_y(-by)]
        return remote(wg.at[c, y], dst, wc_send.at[by - 1], wc_recv.at[by - 1], me)

    wd_copy = remote(wg.at[c], wg.at[c], wd_send, wd_recv, moved(me, 1, 1))
    wd_arrival = remote(wg.at[1 - c], wg.at[1 - c], wd_send, wd_recv, me)
    load_w = pltpu.make_async_copy(wg, w, w_sem)

    def x_copy(j, by, arriving=False):
        send, recv = x_send.at[j, by - 1], x_recv.at[j, by - 1]
        if arriving:
            return remote(sl.at[j, by], xb.at[j, at_x(-by)], send, recv, me)
        return remote(sl.at[j, by], xb.at[j, x], send, recv, moved(me, 2, by))

    def x_start(j):
        for by in (1, 3, 2):
            x_copy(j, by).start()

    def x_wait(j):
        for by in (1, 3, 2):
            x_copy(j, by, arriving=True).wait_recv()

    def z_copy(d, i, g=0, arriving=False):
        if i < 2:
            src = sl.at[2 * i + d, 0] if g == 0 else xb.at[2 * i + d, at_x(-g)]
            dst = zr.at[d, i, at_x(-g)]
        elif i < final:
            src, dst = zs.at[d, i - 2], zr.at[d, i]
        else:
            piece = pl.ds(*PIECES[g])
            src, dst = zs.at[d, i - 2, piece], zr.at[d, i, piece]
        target = me if arriving else moved(me, 3, 1 - 2 * d)
        at = Z_SEM[i] + g
        return remote(src, dst, z_send.at[d, at], z_recv.at[d, at], target)

    def pieces(i):
        return range(NX if i < 2 else 1 if i < final else len(PIECES))

    def placed(at_dest, at_sender, piece, k, r):
        total = None
        for xs in range(NX):
            mine = ibs[at_dest, pl.ds(xs * NZ + at_sender, 1), :] == k
            term = jnp.where(mine, piece(xs)[pl.ds(r, rows), :].astype(F32), 0.0)
            total = term if total is None else total + term
        return total

    def each_part(first, number, body):
        def step(n, _):
            k = first + n // (block // rows)
            r = pl.multiple_of(lax.rem(n, block // rows) * rows, rows)
            body(k, r)
            return 0

        lax.fori_loop(0, number * (block // rows), step, 0)

    def combine(d, i):
        sign = 1 - 2 * d
        dest = at_z(sign * DIST[i])

        def body(k, r):
            total = placed(dest, z, lambda xs: xb.at[2 * i + d, xs], k, r)
            if i < 4:
                total += placed(dest, at_z(-sign), lambda xs: zr.at[d, i - 2, xs], k, r)
            else:
                total += zr[d, i - 2, k, pl.ds(r, rows), :].astype(F32)
            zs[d, i - 2, k, pl.ds(r, rows), :] = total.astype(BF16)

        each_part(0, blocks, body)

    def transpose_feats():
        def one(n, _):
            at = pl.ds(pl.multiple_of(n * block, block), block)
            left[0, :, at] = feats[at, :].T
            return 0

        lax.fori_loop(0, blocks, one, 0)

    def own_product():
        def one(n, _):
            both = jnp.concatenate([w[0, 2 * n], w[0, 2 * n + 1]], axis=1)
            value = jnp.dot(feats[...], both, preferred_element_type=F32)
            pre_own[n] = value
            return 0

        lax.fori_loop(0, NY // 2, one, 0)

    for j in range(2):
        x_start(j)
    for by in range(1, NZ):
        ib_copy(by).start()
    for side, ref in ((0, w_self), (1, w_neigh)):

        @pl.when(c == side)
        def _(ref=ref):
            w_local(ref).start()
            for by in range(1, NZ):
                wa_copy(ref, by).start()

    slots(3)
    slots(-3)
    for j in range(2, 4):
        x_start(j)

    for i in range(last):
        if i < 2:
            for d in (0, 1):
                z_copy(d, i).start()
            for by in (1, 3, 2):
                for d in (0, 1):
                    x_copy(2 * i + d, by, arriving=True).wait_recv()
                    z_copy(d, i, by).start()
        else:
            for d in (0, 1):
                x_wait(2 * i + d)
                for g in pieces(i - 2):
                    z_copy(d, i - 2, g, arriving=True).wait_recv()
                combine(d, i)
            for g in pieces(i):
                for d in (0, 1):
                    z_copy(d, i, g).start()
        if 2 * i + 5 < len(ITEMS):
            x_start(2 * i + 4)
            x_start(2 * i + 5)
        if i == 0:
            slots(2)
            slots(-2)
            w_local(w_self).wait()
            for by in range(1, NZ):
                wa_copy(w_self, by).wait_send()
                wa_arrival(by).wait_recv()
            for by in range(1, NX):
                wb_copy(by).start()
            for by in range(1, NZ):
                ib_arrival(by).wait_recv()
        if i == 1:
            slots(1)
            slots(-1)
            slots(0)
            for by in range(1, NX):
                wb_arrival(by).wait_recv()
            for by in range(1, NY):
                wc_copy(by).start()
        if i == 2:
            transpose_feats()
        if i == 4:
            for by in range(1, NY):
                wc_arrival(by).wait_recv()
            wd_copy.start()
        if i == 5:
            wd_arrival.wait_recv()
            load_w.start()
            load_w.wait()
            own_product()

    load_cot.wait()
    x_wait(2 * last)
    x_wait(2 * last + 1)
    for d in (0, 1):
        z_copy(d, final - 1, arriving=True).wait_recv()

    def swap(g, which, target):
        here = pl.ds(PIECES[g][0] * block, PIECES[g][1] * block)
        if which == 0:
            src, dst = left.at[1 - c, :, here], lp.at[:, here]
            return remote(src, dst, l_send.at[g], l_recv.at[g], target)
        return remote(grad.at[:, here], gp.at[:, here], c_send.at[g], c_recv.at[g], target)

    partner = moved(me, 1, 1)
    scale = 0.7978845608
    for g, (first, number) in enumerate(PIECES):
        for d in (0, 1):
            z_copy(d, final, g, arriving=True).wait_recv()
        for h in (0, 1):

            def body(k, r, h=h, first=first):
                total = placed(z, z, lambda xs: xb.at[2 * last + h, xs], k, r)
                total += zr[h, final, k, pl.ds(r, rows), :].astype(F32)
                total += zr[1 - h, final - 1, k, pl.ds(r, rows), :].astype(F32)
                at = pl.multiple_of((k - first) * block + r, rows)
                agg[pl.ds(at, rows), h * half:(h + 1) * half] = total.astype(BF16)

            each_part(first, number, body)
        span = number * block
        here = pl.ds(first * block, span)
        left[1, :, here] = agg[:span].T

        def gradient(n, _, here=here, span=span):
            both = jnp.concatenate([w[1, 2 * n], w[1, 2 * n + 1]], axis=1)
            pre = pre_own[n, here, :]
            pre += jnp.dot(agg[:span], both, preferred_element_type=F32)
            square = pre * pre
            t = jnp.tanh(scale * (pre + 0.044715 * (square * pre)))
            slope = 0.5 * (1.0 + t)
            slope += (0.5 * scale) * pre * (1.0 - t * t) * (1.0 + 0.134145 * square)
            columns = pl.ds(pl.multiple_of(n * 2 * chunk, 2 * chunk), 2 * chunk)
            grad[n, here, :] = (cot[here, columns].astype(F32) * slope).astype(BF16)
            return 0

        lax.fori_loop(0, NY // 2, gradient, 0)
        for which in (0, 1):
            swap(g, which, partner).start()

    own = (own0, own1, own2)
    parts = (own, (mid0, mid1, mid2), (low0, low1, low2))
    inbox = ((a0, a1, a2), (b0, b1, b2), (d0, d1, d2))
    width = lp.shape[0]

    def own_terms(n, _):
        pre_own[n, :width, :] = jnp.dot(left[c], grad[n], preferred_element_type=F32)
        return 0

    lax.fori_loop(0, NY // 2, own_terms, 0)
    for g in range(len(PIECES)):
        for which in (0, 1):
            swap(g, which, me).wait_recv()

    def hop(j, s, by, arriving=False):
        axis = ORDER[j][s]
        size = SIZES[axis]
        at = me[axis]
        src = parts[s][j].at[lax.rem(at + by, size)]
        send, recv = s_send.at[s, j, by - 1], s_recv.at[s, j, by - 1]
        if arriving:
            return remote(src, inbox[s][j].at[lax.rem(at + size - by, size)], send, recv, me)
        return remote(src, inbox[s][j].at[at], send, recv, moved(me, axis, by))

    def hops(j, s):
        return range(1, SIZES[ORDER[j][s]])

    def first_hop(j, n, by, arriving=False):
        axis = ORDER[j][0]
        size = SIZES[axis]
        at = me[axis]
        there = lax.rem(at + by, size)
        back = lax.rem(at + size - by, size) if arriving else at
        pair = pl.ds(2 * n, 2)
        if j == 1:
            src, dst = own1.at[there, pair], a1.at[back, pair]
        else:
            src, dst = own2.at[there, :, pair], a2.at[back, :, pair]
        target = me if arriving else moved(me, axis, by)
        return remote(src, dst, f_send.at[j - 1, n, by - 1], f_recv.at[j - 1, n, by - 1], target)

    for n in range(NY // 2):
        both = pre_own[n, :width, :] + jnp.dot(lp[...], gp[n], preferred_element_type=F32)
        for e in range(2):
            v = both[:, e * chunk:(e + 1) * chunk].reshape(NX, NZ, 3, 8, chunk)
            for xs in range(NX):
                own1[:, 2 * n + e, xs] = v[xs, :, 1].astype(BF16)
                own2[xs, :, 2 * n + e] = v[xs, :, 2].astype(BF16)
                own0[2 * n + e, :, xs] = v[xs, :, 0].astype(BF16)
        for j in (1, 2):
            for by in hops(j, 0):
                first_hop(j, n, by).start()
        for there in (2 * n, 2 * n + 1):

            @pl.when(y != there)
            def _(there=there):
                at = lax.rem(there - y + NY, NY) - 1
                target = (there, c, x, z)
                send, recv = s_send.at[0, 0, at], s_recv.at[0, 0, at]
                remote(own0.at[there], a0.at[y], send, recv, target).start()

    def first_hops(j):
        return [(n, by) for n in range(NY // 2) for by in hops(j, 0)]

    for s in range(3):
        for j in (2, 0, 1):
            axis = ORDER[j][s]
            size = SIZES[axis]
            at_axis = me[axis]
            if s == 0 and j > 0:
                for n, by in first_hops(j):
                    first_hop(j, n, by, arriving=True).wait_recv()
            else:
                for by in hops(j, s):
                    hop(j, s, by, arriving=True).wait_recv()

            def total(at, j=j, s=s, at_axis=at_axis, size=size):
                value = parts[s][j][(at_axis, *at)].astype(F32)
                for by in range(1, size):
                    value += inbox[s][j][(lax.rem(at_axis + by, size), *at)].astype(F32)
                return value

            if s == 2:
                every[c, y, j] = total(()).astype(BF16)
                continue

            def add(n, _, j=j, s=s, total=total):
                parts[s + 1][j][n] = total((n,)).astype(BF16)
                return 0

            lax.fori_loop(0, parts[s + 1][j].shape[0], add, 0)
            for by in hops(j, s + 1):
                hop(j, s + 1, by).start()

    others = [(by, core) for by in range(NY) for core in range(NC) if by or core]

    def gather(at, arriving=False):
        by, core = others[at]
        dst = every.at[c, y]
        target = me
        if arriving:
            dst = every.at[lax.rem(c + core, NC), at_y(-by)]
        else:
            target = moved(moved(me, 0, by), 1, core)
        return remote(every.at[c, y], dst, g_send.at[at], g_recv.at[at], target)

    for at in range(len(others)):
        gather(at).start()
    for at in range(len(others)):
        gather(at, arriving=True).wait_recv()
    for side in (0, 1):
        for n in range(NY):
            for j in range(3):
                out[side, j * 8:(j + 1) * 8, n * chunk:(n + 1) * chunk] = every[side, n, j].astype(F32)

    for at in range(len(others)):
        gather(at).wait_send()
    wd_copy.wait_send()
    for by in range(1, NZ):
        ib_copy(by).wait_send()
    for by in range(1, NX):
        wb_copy(by).wait_send()
    for by in range(1, NY):
        wc_copy(by).wait_send()
    for j in range(len(ITEMS)):
        for by in range(1, NX):
            x_copy(j, by).wait_send()
    for i in range(last):
        for d in (0, 1):
            for g in pieces(i):
                z_copy(d, i, g).wait_send()
    for g in range(len(PIECES)):
        for which in (0, 1):
            swap(g, which, partner).wait_send()
    for j in range(3):
        for s in range(3):
            if s == 0 and j > 0:
                for n, by in first_hops(j):
                    first_hop(j, n, by).wait_send()
            else:
                for by in hops(j, s):
                    hop(j, s, by).wait_send()


def shards(features, cotangent, w_self, w_neigh, tile_vals, tile_src, tile_peer, in_block):
    count, block, _ = tile_vals.shape
    nodes, width = features.shape
    half = width // 2
    owned, hidden = w_self.shape
    blocks = nodes // block
    chunk = hidden // NY

    key = tile_peer * blocks + tile_src
    order = jnp.arange(count, dtype=jnp.int32)
    wanted = jnp.concatenate([key, jnp.arange(NDOM * blocks, dtype=jnp.int32)])
    limit = jnp.concatenate([order, jnp.full((NDOM * blocks,), count, jnp.int32)])
    found = (wanted[:, None] == key[None, :]) & (order[None, :] < limit[:, None])
    idx = jnp.max(jnp.where(found, order[None, :], -1), axis=1)
    idx = jnp.where(idx < 0, count, idx)

    dma = pltpu.SemaphoreType.DMA
    vmem = pl.BlockSpec(memory_space=pltpu.VMEM)
    smem = pl.BlockSpec(memory_space=pltpu.SMEM)
    anywhere = pl.BlockSpec(memory_space=pl.ANY)
    steps = len(DIST)
    items = len(ITEMS)
    thirds = [(NY, NZ, NX, 8, chunk), (NZ, NY, NX, 8, chunk), (NX, NZ, NY, 8, chunk)]
    scratch = [
        pltpu.VMEM((count + 1, block, block), F32),
        pltpu.VMEM((items, NX, block, half), BF16),
        pltpu.VMEM((items, NX, block, half), BF16),
        pltpu.VMEM((2, steps, blocks, block, half), BF16),
        pltpu.VMEM((2, steps - 2, blocks, block, half), BF16),
        pltpu.VMEM((NZ, NDOM, half), jnp.int32),
        pltpu.VMEM((nodes, hidden), BF16),
        pltpu.VMEM((NC, NY, width, chunk), BF16),
        pltpu.VMEM((NY // 2, nodes, 2 * chunk), F32),
        pltpu.VMEM((max(n for _, n in PIECES) * block, width), BF16),
        pltpu.VMEM((2, width, nodes), BF16),
        pltpu.VMEM((NY // 2, nodes, 2 * chunk), BF16),
        pltpu.VMEM((width, nodes), BF16),
        pltpu.VMEM((NY // 2, nodes, 2 * chunk), BF16),
    ]
    for skip in (0, 1, 2, 0, 1, 2):
        scratch += [pltpu.VMEM(t[skip:], BF16) for t in thirds]
    scratch += [
        pltpu.VMEM((NC, NY, 3, 8, chunk), BF16),
        dma((items, NX - 1)),
        dma((items, NX - 1)),
        dma((2, Z_SEM[-1] + len(PIECES))),
        dma((2, Z_SEM[-1] + len(PIECES))),
        dma((NZ - 1,)),
        dma((NZ - 1,)),
        dma,
        dma,
        dma((NZ - 1,)),
        dma((NZ - 1,)),
        dma,
        dma((NX - 1,)),
        dma((NX - 1,)),
        dma((NY - 1,)),
        dma((NY - 1,)),
        dma,
        dma,
        dma((len(PIECES),)),
        dma((len(PIECES),)),
        dma((len(PIECES),)),
        dma((len(PIECES),)),
        dma((2, NY // 2, 7)),
        dma((2, NY // 2, 7)),
        dma((3, 3, 7)),
        dma((3, 3, 7)),
        dma((NY * NC - 1,)),
        dma((NY * NC - 1,)),
    ]
    out, _ = pl.pallas_call(
        step_kernel,
        out_shape=(
            jax.ShapeDtypeStruct((NC, owned, hidden), F32),
            jax.ShapeDtypeStruct((NC, NY, width, chunk), BF16),
        ),
        in_specs=[smem, smem, vmem, vmem, anywhere, anywhere, anywhere],
        out_specs=(vmem, anywhere),
        scratch_shapes=scratch,
        compiler_params=pltpu.CompilerParams(
            collective_id=0, has_side_effects=True, vmem_limit_bytes=VMEM_BYTES
        ),
        name="step",
    )(idx, in_block, tile_vals, features, cotangent, w_self, w_neigh)
    return out[0], out[1]


def solution(mesh):
    split = Mesh(mesh.devices.reshape(SIZES), AXES)
    every = P(AXES)
    rows = P(AXES, None)
    placed = (
        rows,
        rows,
        P(("x", "z"), None),
        P(("x", "z"), None),
        P(AXES, None, None),
        every,
        every,
        every,
    )
    out = P(("x", "z"), None)
    return jax.shard_map(
        shards, mesh=split, in_specs=placed, out_specs=(out, out), check_vma=False
    )
```

```python
import functools

import jax
import jax.numpy as jnp
from jax import lax
from jax.experimental import pallas as pl
from jax.experimental.pallas import tpu as pltpu
from jax.sharding import Mesh
from jax.sharding import PartitionSpec as P

AXES = ("y", "c", "x", "z")
SIZES = (8, 2, 4, 8)
NY, NC, NX, NZ = SIZES
NDOM = NX * NZ
MESH = pl.DeviceIdType.MESH
VMEM_BYTES = 67043328
F32 = jnp.float32
BF16 = jnp.bfloat16

DIST = (4, 3, 3, 2, 2, 1, 1)
PIECES = ((0, 2), (2, 2), (4, 2), (6, 1), (7, 1))
Z_SEM = (0, 4, 8, 9, 10, 11, 12)
ITEMS = []
for _i, _d in enumerate(DIST):
    ITEMS += [(_i % 2, _d), (1 - _i % 2, -_d)]
ITEMS += [(0, 0), (1, 0)]


def position():
    return tuple(lax.axis_index(a) for a in AXES)


def moved(me, axis, by):
    return tuple(
        lax.rem(m + (by % SIZES[axis]), SIZES[axis]) if a == axis else m
        for a, m in enumerate(me)
    )


def greet(me):
    barrier = pltpu.get_barrier_semaphore()
    count = 0
    for axis, size in enumerate(SIZES):
        for by in range(1, size):
            pl.semaphore_signal(
                barrier, inc=1, device_id=moved(me, axis, by), device_id_type=MESH
            )
            count += 1
    for by in range(1, NY):
        other = moved(moved(me, 0, by), 1, 1)
        pl.semaphore_signal(barrier, inc=1, device_id=other, device_id_type=MESH)
        count += 1
    pl.semaphore_wait(barrier, count)


def remote(src, dst, send, recv, target):
    return pltpu.make_async_remote_copy(
        src_ref=src, dst_ref=dst, send_sem=send, recv_sem=recv,
        device_id=target, device_id_type=MESH,
    )


ORDER = ((0, 3, 2), (3, 0, 2), (2, 3, 0))


def step_kernel(
    idx, inb, tiles, feats, cot_in, w_self, w_neigh, out, wg,
    ct, sl, xb, zr, zs, ibs, cot, w, pre_own, agg, left, grad,
    lp, gp, own0, own1, own2, mid0, mid1, mid2, low0, low1, low2,
    a0, a1, a2, b0, b1, b2, d0, d1, d2, every,
    x_send, x_recv, z_send, z_recv, ib_send, ib_recv, cot_sem, w_sem,
    wa_send, wa_recv, w_own, wb_send, wb_recv, wc_send, wc_recv, wd_send, wd_recv,
    l_send, l_recv, c_send, c_recv, f_send, f_recv, s_send, s_recv, g_send, g_recv,
):
    me = position()
    y, c, x, z = me
    block, half = xb.shape[2], xb.shape[3]
    blocks = zr.shape[2]
    owned = w_self.shape[0]
    chunk = wg.shape[3]
    count = tiles.shape[0]
    rows = 32
    last = len(DIST)
    final = last - 1

    def at_z(by):
        return lax.rem(z + (by % NZ), NZ)

    def at_x(by):
        return lax.rem(x + (by % NX), NX)

    def at_y(by):
        return lax.rem(y + (by % NY), NY)

    for s in range(NDOM):
        ibs[z, s:s + 1, :] = jnp.full((1, half), inb[s], jnp.int32)
    load_cot = pltpu.make_async_copy(cot_in, cot, cot_sem)
    load_cot.start()
    ct[...] = jnp.zeros_like(ct)

    def chain(t, _):
        ct[t] = tiles[t].astype(F32) + ct[idx[t]]
        return 0

    lax.fori_loop(0, count, chain, 0)

    def slots(rel):
        j0, j1 = (
            next(j for j, (h, at) in enumerate(ITEMS) if h == side and (at - rel) % NZ == 0)
            for side in (0, 1)
        )

        def one(by, _):
            p = lax.rem(x + by, NX) * NZ + at_z(rel)
            parts = [ct[idx[count + p * blocks + b]].astype(BF16) for b in range(blocks)]
            value = jnp.dot(jnp.concatenate(parts, axis=1), feats[...], preferred_element_type=F32)
            sl[j0, by] = value[:, :half].astype(BF16)
            sl[j1, by] = value[:, half:].astype(BF16)
            return 0

        lax.fori_loop(0, NX, one, 0)
        xb[j0, x] = sl[j0, 0]
        xb[j1, x] = sl[j1, 0]

    slots(4)
    greet(me)

    def ib_copy(by):
        ref = ibs.at[z]
        return remote(ref, ref, ib_send.at[by - 1], ib_recv.at[by - 1], moved(me, 3, by))

    def ib_arrival(by):
        return remote(ibs.at[z], ibs.at[at_z(-by)], ib_send.at[by - 1], ib_recv.at[by - 1], me)

    def wg_rows(at, size):
        return wg.at[c, y, pl.ds(pl.multiple_of(at * owned, owned), size * owned)]

    def w_src(ref):
        return ref.at[:, pl.ds(pl.multiple_of(y * chunk, chunk), chunk)]

    def w_local(ref):
        return pltpu.make_async_copy(w_src(ref), wg_rows(x * NZ + z, 1), w_own)

    def wa_copy(ref, by):
        dst = wg_rows(x * NZ + z, 1)
        return remote(w_src(ref), dst, wa_send.at[by - 1], wa_recv.at[by - 1], moved(me, 3, by))

    def wa_arrival(by):
        dst = wg_rows(x * NZ + at_z(-by), 1)
        return remote(w_src(w_self), dst, wa_send.at[by - 1], wa_recv.at[by - 1], me)

    def wb_copy(by):
        ref = wg_rows(x * NZ, NZ)
        return remote(ref, ref, wb_send.at[by - 1], wb_recv.at[by - 1], moved(me, 2, by))

    def wb_arrival(by):
        dst = wg_rows(at_x(-by) * NZ, NZ)
        return remote(wg_rows(x * NZ, NZ), dst, wb_send.at[by - 1], wb_recv.at[by - 1], me)

    def wc_copy(by):
        ref = wg.at[c, y]
        return remote(ref, ref, wc_send.at[by - 1], wc_recv.at[by - 1], moved(me, 0, by))

    def wc_arrival(by):
        dst = wg.at[c, at_y(-by)]
        return remote(wg.at[c, y], dst, wc_send.at[by - 1], wc_recv.at[by - 1], me)

    wd_copy = remote(wg.at[c], wg.at[c], wd_send, wd_recv, moved(me, 1, 1))
    wd_arrival = remote(wg.at[1 - c], wg.at[1 - c], wd_send, wd_recv, me)
    load_w = pltpu.make_async_copy(wg, w, w_sem)

    def x_copy(j, by, arriving=False):
        send, recv = x_send.at[j, by - 1], x_recv.at[j, by - 1]
        if arriving:
            return remote(sl.at[j, by], xb.at[j, at_x(-by)], send, recv, me)
        return remote(sl.at[j, by], xb.at[j, x], send, recv, moved(me, 2, by))

    def x_start(j):
        for by in (1, 3, 2):
            x_copy(j, by).start()

    def x_wait(j):
        for by in (1, 3, 2):
            x_copy(j, by, arriving=True).wait_recv()

    def z_copy(d, i, g=0, arriving=False):
        if i < 2:
            src = sl.at[2 * i + d, 0] if g == 0 else xb.at[2 * i + d, at_x(-g)]
            dst = zr.at[d, i, at_x(-g)]
        elif i < final:
            src, dst = zs.at[d, i - 2], zr.at[d, i]
        else:
            piece = pl.ds(*PIECES[g])
            src, dst = zs.at[d, i - 2, piece], zr.at[d, i, piece]
        target = me if arriving else moved(me, 3, 1 - 2 * d)
        at = Z_SEM[i] + g
        return remote(src, dst, z_send.at[d, at], z_recv.at[d, at], target)

    def pieces(i):
        return range(NX if i < 2 else 1 if i < final else len(PIECES))

    def placed(at_dest, at_sender, piece, k, r):
        total = None
        for xs in range(NX):
            mine = ibs[at_dest, pl.ds(xs * NZ + at_sender, 1), :] == k
            term = jnp.where(mine, piece(xs)[pl.ds(r, rows), :].astype(F32), 0.0)
            total = term if total is None else total + term
        return total

    def each_part(first, number, body):
        def step(n, _):
            k = first + n // (block // rows)
            r = pl.multiple_of(lax.rem(n, block // rows) * rows, rows)
            body(k, r)
            return 0

        lax.fori_loop(0, number * (block // rows), step, 0)

    def combine(d, i):
        sign = 1 - 2 * d
        dest = at_z(sign * DIST[i])

        def body(k, r):
            total = placed(dest, z, lambda xs: xb.at[2 * i + d, xs], k, r)
            if i < 4:
                total += placed(dest, at_z(-sign), lambda xs: zr.at[d, i - 2, xs], k, r)
            else:
                total += zr[d, i - 2, k, pl.ds(r, rows), :].astype(F32)
            zs[d, i - 2, k, pl.ds(r, rows), :] = total.astype(BF16)

        each_part(0, blocks, body)

    def transpose_feats():
        def one(n, _):
            at = pl.ds(pl.multiple_of(n * block, block), block)
            left[0, :, at] = feats[at, :].T
            return 0

        lax.fori_loop(0, blocks, one, 0)

    def own_product():
        def one(n, _):
            both = jnp.concatenate([w[0, 2 * n], w[0, 2 * n + 1]], axis=1)
            value = jnp.dot(feats[...], both, preferred_element_type=F32)
            pre_own[n] = value
            return 0

        lax.fori_loop(0, NY // 2, one, 0)

    for j in range(2):
        x_start(j)
    for by in range(1, NZ):
        ib_copy(by).start()
    for side, ref in ((0, w_self), (1, w_neigh)):

        @pl.when(c == side)
        def _(ref=ref):
            w_local(ref).start()
            for by in range(1, NZ):
                wa_copy(ref, by).start()

    slots(3)
    slots(-3)
    for j in range(2, 4):
        x_start(j)

    for i in range(last):
        if i < 2:
            for d in (0, 1):
                z_copy(d, i).start()
            for by in (1, 3, 2):
                for d in (0, 1):
                    x_copy(2 * i + d, by, arriving=True).wait_recv()
                    z_copy(d, i, by).start()
        else:
            for d in (0, 1):
                x_wait(2 * i + d)
                for g in pieces(i - 2):
                    z_copy(d, i - 2, g, arriving=True).wait_recv()
                combine(d, i)
            for g in pieces(i):
                for d in (0, 1):
                    z_copy(d, i, g).start()
        for j in range(4, 8) if i == 1 else range(2 * i + 4, 2 * i + 6) if i > 1 else ():
            if j < len(ITEMS):
                x_start(j)
        if i == 0:
            slots(2)
            slots(-2)
            w_local(w_self).wait()
            for by in range(1, NZ):
                wa_copy(w_self, by).wait_send()
                wa_arrival(by).wait_recv()
            for by in range(1, NX):
                wb_copy(by).start()
            for by in range(1, NZ):
                ib_arrival(by).wait_recv()
        if i == 1:
            slots(1)
            slots(-1)
            slots(0)
            for by in range(1, NX):
                wb_arrival(by).wait_recv()
            for by in range(1, NY):
                wc_copy(by).start()
        if i == 2:
            transpose_feats()
        if i == 4:
            for by in range(1, NY):
                wc_arrival(by).wait_recv()
            wd_copy.start()
        if i == 5:
            wd_arrival.wait_recv()
            load_w.start()
            load_w.wait()
            own_product()

    load_cot.wait()
    x_wait(2 * last)
    x_wait(2 * last + 1)
    for d in (0, 1):
        z_copy(d, final - 1, arriving=True).wait_recv()

    def swap(g, which, target):
        here = pl.ds(PIECES[g][0] * block, PIECES[g][1] * block)
        if which == 0:
            src, dst = left.at[1 - c, :, here], lp.at[:, here]
            return remote(src, dst, l_send.at[g], l_recv.at[g], target)
        return remote(grad.at[:, here], gp.at[:, here], c_send.at[g], c_recv.at[g], target)

    partner = moved(me, 1, 1)
    scale = 0.7978845608
    for g, (first, number) in enumerate(PIECES):
        for d in (0, 1):
            z_copy(d, final, g, arriving=True).wait_recv()
        for h in (0, 1):

            def body(k, r, h=h, first=first):
                total = placed(z, z, lambda xs: xb.at[2 * last + h, xs], k, r)
                total += zr[h, final, k, pl.ds(r, rows), :].astype(F32)
                total += zr[1 - h, final - 1, k, pl.ds(r, rows), :].astype(F32)
                at = pl.multiple_of((k - first) * block + r, rows)
                agg[pl.ds(at, rows), h * half:(h + 1) * half] = total.astype(BF16)

            each_part(first, number, body)
        span = number * block
        here = pl.ds(first * block, span)
        left[1, :, here] = agg[:span].T

        def gradient(n, _, here=here, span=span):
            both = jnp.concatenate([w[1, 2 * n], w[1, 2 * n + 1]], axis=1)
            pre = pre_own[n, here, :]
            pre += jnp.dot(agg[:span], both, preferred_element_type=F32)
            square = pre * pre
            t = jnp.tanh(scale * (pre + 0.044715 * (square * pre)))
            slope = 0.5 * (1.0 + t)
            slope += (0.5 * scale) * pre * (1.0 - t * t) * (1.0 + 0.134145 * square)
            columns = pl.ds(pl.multiple_of(n * 2 * chunk, 2 * chunk), 2 * chunk)
            grad[n, here, :] = (cot[here, columns].astype(F32) * slope).astype(BF16)
            return 0

        lax.fori_loop(0, NY // 2, gradient, 0)
        for which in (0, 1):
            swap(g, which, partner).start()

    own = (own0, own1, own2)
    parts = (own, (mid0, mid1, mid2), (low0, low1, low2))
    inbox = ((a0, a1, a2), (b0, b1, b2), (d0, d1, d2))
    width = lp.shape[0]

    def own_terms(n, _):
        pre_own[n, :width, :] = jnp.dot(left[c], grad[n], preferred_element_type=F32)
        return 0

    lax.fori_loop(0, NY // 2, own_terms, 0)
    for g in range(len(PIECES)):
        for which in (0, 1):
            swap(g, which, me).wait_recv()

    def hop(j, s, by, arriving=False):
        axis = ORDER[j][s]
        size = SIZES[axis]
        at = me[axis]
        src = parts[s][j].at[lax.rem(at + by, size)]
        send, recv = s_send.at[s, j, by - 1], s_recv.at[s, j, by - 1]
        if arriving:
            return remote(src, inbox[s][j].at[lax.rem(at + size - by, size)], send, recv, me)
        return remote(src, inbox[s][j].at[at], send, recv, moved(me, axis, by))

    def hops(j, s):
        return range(1, SIZES[ORDER[j][s]])

    def first_hop(j, n, by, arriving=False):
        axis = ORDER[j][0]
        size = SIZES[axis]
        at = me[axis]
        there = lax.rem(at + by, size)
        back = lax.rem(at + size - by, size) if arriving else at
        pair = pl.ds(2 * n, 2)
        if j == 1:
            src, dst = own1.at[there, pair], a1.at[back, pair]
        else:
            src, dst = own2.at[there, :, pair], a2.at[back, :, pair]
        target = me if arriving else moved(me, axis, by)
        return remote(src, dst, f_send.at[j - 1, n, by - 1], f_recv.at[j - 1, n, by - 1], target)

    for n in range(NY // 2):
        both = pre_own[n, :width, :] + jnp.dot(lp[...], gp[n], preferred_element_type=F32)
        for e in range(2):
            v = both[:, e * chunk:(e + 1) * chunk].reshape(NX, NZ, 3, 8, chunk)
            for xs in range(NX):
                own1[:, 2 * n + e, xs] = v[xs, :, 1].astype(BF16)
                own2[xs, :, 2 * n + e] = v[xs, :, 2].astype(BF16)
                own0[2 * n + e, :, xs] = v[xs, :, 0].astype(BF16)
        for j in (1, 2):
            for by in hops(j, 0):
                first_hop(j, n, by).start()
        for there in (2 * n, 2 * n + 1):

            @pl.when(y != there)
            def _(there=there):
                at = lax.rem(there - y + NY, NY) - 1
                target = (there, c, x, z)
                send, recv = s_send.at[0, 0, at], s_recv.at[0, 0, at]
                remote(own0.at[there], a0.at[y], send, recv, target).start()

    def first_hops(j):
        return [(n, by) for n in range(NY // 2) for by in hops(j, 0)]

    for s in range(3):
        for j in (2, 0, 1):
            axis = ORDER[j][s]
            size = SIZES[axis]
            at_axis = me[axis]
            if s == 0 and j > 0:
                for n, by in first_hops(j):
                    first_hop(j, n, by, arriving=True).wait_recv()
            else:
                for by in hops(j, s):
                    hop(j, s, by, arriving=True).wait_recv()

            def total(at, j=j, s=s, at_axis=at_axis, size=size):
                value = parts[s][j][(at_axis, *at)].astype(F32)
                for by in range(1, size):
                    value += inbox[s][j][(lax.rem(at_axis + by, size), *at)].astype(F32)
                return value

            if s == 2:
                every[c, y, j] = total(()).astype(BF16)
                continue

            def add(n, _, j=j, s=s, total=total):
                parts[s + 1][j][n] = total((n,)).astype(BF16)
                return 0

            lax.fori_loop(0, parts[s + 1][j].shape[0], add, 0)
            for by in hops(j, s + 1):
                hop(j, s + 1, by).start()

    others = [(by, core) for by in range(NY) for core in range(NC) if by or core]

    def gather(at, arriving=False):
        by, core = others[at]
        dst = every.at[c, y]
        target = me
        if arriving:
            dst = every.at[lax.rem(c + core, NC), at_y(-by)]
        else:
            target = moved(moved(me, 0, by), 1, core)
        return remote(every.at[c, y], dst, g_send.at[at], g_recv.at[at], target)

    for at in range(len(others)):
        gather(at).start()
    for at in range(len(others)):
        gather(at, arriving=True).wait_recv()
    for side in (0, 1):
        for n in range(NY):
            for j in range(3):
                out[side, j * 8:(j + 1) * 8, n * chunk:(n + 1) * chunk] = every[side, n, j].astype(F32)

    for at in range(len(others)):
        gather(at).wait_send()
    wd_copy.wait_send()
    for by in range(1, NZ):
        ib_copy(by).wait_send()
    for by in range(1, NX):
        wb_copy(by).wait_send()
    for by in range(1, NY):
        wc_copy(by).wait_send()
    for j in range(len(ITEMS)):
        for by in range(1, NX):
            x_copy(j, by).wait_send()
    for i in range(last):
        for d in (0, 1):
            for g in pieces(i):
                z_copy(d, i, g).wait_send()
    for g in range(len(PIECES)):
        for which in (0, 1):
            swap(g, which, partner).wait_send()
    for j in range(3):
        for s in range(3):
            if s == 0 and j > 0:
                for n, by in first_hops(j):
                    first_hop(j, n, by).wait_send()
            else:
                for by in hops(j, s):
                    hop(j, s, by).wait_send()


def shards(features, cotangent, w_self, w_neigh, tile_vals, tile_src, tile_peer, in_block):
    count, block, _ = tile_vals.shape
    nodes, width = features.shape
    half = width // 2
    owned, hidden = w_self.shape
    blocks = nodes // block
    chunk = hidden // NY

    key = tile_peer * blocks + tile_src
    order = jnp.arange(count, dtype=jnp.int32)
    wanted = jnp.concatenate([key, jnp.arange(NDOM * blocks, dtype=jnp.int32)])
    limit = jnp.concatenate([order, jnp.full((NDOM * blocks,), count, jnp.int32)])
    found = (wanted[:, None] == key[None, :]) & (order[None, :] < limit[:, None])
    idx = jnp.max(jnp.where(found, order[None, :], -1), axis=1)
    idx = jnp.where(idx < 0, count, idx)

    dma = pltpu.SemaphoreType.DMA
    vmem = pl.BlockSpec(memory_space=pltpu.VMEM)
    smem = pl.BlockSpec(memory_space=pltpu.SMEM)
    anywhere = pl.BlockSpec(memory_space=pl.ANY)
    steps = len(DIST)
    items = len(ITEMS)
    thirds = [(NY, NZ, NX, 8, chunk), (NZ, NY, NX, 8, chunk), (NX, NZ, NY, 8, chunk)]
    scratch = [
        pltpu.VMEM((count + 1, block, block), F32),
        pltpu.VMEM((items, NX, block, half), BF16),
        pltpu.VMEM((items, NX, block, half), BF16),
        pltpu.VMEM((2, steps, blocks, block, half), BF16),
        pltpu.VMEM((2, steps - 2, blocks, block, half), BF16),
        pltpu.VMEM((NZ, NDOM, half), jnp.int32),
        pltpu.VMEM((nodes, hidden), BF16),
        pltpu.VMEM((NC, NY, width, chunk), BF16),
        pltpu.VMEM((NY // 2, nodes, 2 * chunk), F32),
        pltpu.VMEM((max(n for _, n in PIECES) * block, width), BF16),
        pltpu.VMEM((2, width, nodes), BF16),
        pltpu.VMEM((NY // 2, nodes, 2 * chunk), BF16),
        pltpu.VMEM((width, nodes), BF16),
        pltpu.VMEM((NY // 2, nodes, 2 * chunk), BF16),
    ]
    for skip in (0, 1, 2, 0, 1, 2):
        scratch += [pltpu.VMEM(t[skip:], BF16) for t in thirds]
    scratch += [
        pltpu.VMEM((NC, NY, 3, 8, chunk), BF16),
        dma((items, NX - 1)),
        dma((items, NX - 1)),
        dma((2, Z_SEM[-1] + len(PIECES))),
        dma((2, Z_SEM[-1] + len(PIECES))),
        dma((NZ - 1,)),
        dma((NZ - 1,)),
        dma,
        dma,
        dma((NZ - 1,)),
        dma((NZ - 1,)),
        dma,
        dma((NX - 1,)),
        dma((NX - 1,)),
        dma((NY - 1,)),
        dma((NY - 1,)),
        dma,
        dma,
        dma((len(PIECES),)),
        dma((len(PIECES),)),
        dma((len(PIECES),)),
        dma((len(PIECES),)),
        dma((2, NY // 2, 7)),
        dma((2, NY // 2, 7)),
        dma((3, 3, 7)),
        dma((3, 3, 7)),
        dma((NY * NC - 1,)),
        dma((NY * NC - 1,)),
    ]
    out, _ = pl.pallas_call(
        step_kernel,
        out_shape=(
            jax.ShapeDtypeStruct((NC, owned, hidden), F32),
            jax.ShapeDtypeStruct((NC, NY, width, chunk), BF16),
        ),
        in_specs=[smem, smem, vmem, vmem, anywhere, anywhere, anywhere],
        out_specs=(vmem, anywhere),
        scratch_shapes=scratch,
        compiler_params=pltpu.CompilerParams(
            collective_id=0, has_side_effects=True, vmem_limit_bytes=VMEM_BYTES
        ),
        name="step",
    )(idx, in_block, tile_vals, features, cotangent, w_self, w_neigh)
    return out[0], out[1]


def solution(mesh):
    split = Mesh(mesh.devices.reshape(SIZES), AXES)
    every = P(AXES)
    rows = P(AXES, None)
    placed = (
        rows,
        rows,
        P(("x", "z"), None),
        P(("x", "z"), None),
        P(AXES, None, None),
        every,
        every,
        every,
    )
    out = P(("x", "z"), None)
    return jax.shard_map(
        shards, mesh=split, in_specs=placed, out_specs=(out, out), check_vma=False
    )
```
